32 devices in a mesh: chan: 4 (over y, core), blk: 8 (over z, x).
Axes of the slice: x: 2, y: 2, z: 4, core: 2. Of those that a mesh axis runs over, the one named last changes fastest.
Arguments:
- comp_alms: float32 [3, 4, 8, 4096], P(None, None, 'blk', 'chan'), may hold values from -6 to 6
- legendre: bfloat16 [2, 8, 4096, 32], P(None, 'blk'), may hold values from -0.09375 to 0.09375
- inv_noise: float32 [4, 2, 32, 8192], P('chan', None, 'blk'), may hold values from 0.5 to 5
- beam_window: float32 [4, 4096], replicated, may hold values from 0.1 to 1
- mixing: float32 [4, 3], replicated, may hold values from 0.2 to 1.5
- channel_of: int32 [4], replicated, may hold values from 0 to 3, each once
- m_orders: int32 [8], replicated, may hold values from 0 to 4095, as said below
- cycle_of: int32 [32], replicated, may hold values from 0 to 31, each once
- cycle_pixels: int32 [32], replicated, may hold values from 4 to 8192, as said below
Outputs:
- normal_product: float32 [3, 4, 8, 4096], P(None, None, 'blk', 'chan')
The draws below stay inside these ranges and needn't reach their ends.
Inputs may be any that keep to these rules, and one draw needn't show every extreme that they name: `m_orders`: the orders are distinct. `cycle_pixels`: each entry is 4 * min(h, 2048, 8192 - h) for some cycle number h of 1 to 8191; at least one entry equals 8192.
All inputs are finite; a program needn't handle non-finite values.
Results may differ from the reference program's by a relative error of at most 0.0022.
Values may be sent and summed in bfloat16 or wider, within the bound.
A program may use at most 128 MiB of HBM per device.

```python
import math
import jax
import jax.numpy as jnp
from jax import lax

L = 4096
PIX = 8192
NC = 3
CH = 4
M_TOT = 8
R_TOT = 32


def draw_m_orders(key, part):
    return jax.random.permutation(key, L)[:M_TOT].astype(jnp.int32)


def draw_cycle_pixels(key, part):
    first_key, second_key = jax.random.split(jax.random.fold_in(key, 17))
    numbers = jax.random.randint(first_key, (R_TOT,), 1, PIX).astype(jnp.int32)
    position = jax.random.randint(second_key, (), 0, R_TOT)
    numbers = numbers.at[position].set(PIX // 2)
    quarter = PIX // 4
    return (4 * jnp.minimum(jnp.minimum(numbers, quarter), PIX - numbers)).astype(jnp.int32)


def level_of(stream_key, extent, shards, least, high):
    gain = 1.0
    for dim, shards_of in shards:
        heights = jax.random.uniform(jax.random.fold_in(jax.random.fold_in(stream_key, 6), dim), (shards_of,), jnp.float32, least / len(shards), high / len(shards))
        gain = gain * jnp.repeat(jnp.exp(heights), extent[dim] // shards_of).reshape((-1,) + (1,) * (len(extent) - 1 - dim))
    return gain


def normal_values(rng, dims, deviation, bound, cuts=(), held_as=jnp.bfloat16):
    factor_of = level_of(rng, dims, cuts, -0.22, 0.18) if cuts else 1.0
    result = jax.random.normal(rng, dims, jnp.float32) * deviation * factor_of
    return jnp.minimum(jnp.maximum(result, -bound), bound).astype(held_as)


def setup_inputs(seed: int = 0) -> dict:
    key_list = jax.random.split(jax.random.key(seed), 10)
    comp_alms = normal_values(key_list[0], (NC, 4, M_TOT, L), 1.0, 6.0, ((2, 8), (3, 4)), jnp.float32)
    legendre = normal_values(key_list[1], (2, M_TOT, L, R_TOT), L ** -0.5, 0.09375, ((1, 8),))
    inv_noise = jnp.clip(jnp.exp(math.log(5.0) - 2.3025851 * jax.random.uniform(key_list[2], (CH, 2, R_TOT, PIX), jnp.float32) ** level_of(key_list[2], (CH, 2, R_TOT, PIX), ((0, 4), (2, 8)), -0.2, 0.2)), 0.5, 5.0)
    beam_window = jnp.clip(jax.random.uniform(key_list[3], (CH, L), jnp.float32, 0.1, 1.0), 0.1, 1.0)
    mixing = jnp.clip(jax.random.uniform(key_list[4], (CH, NC), jnp.float32, 0.2, 1.5), 0.2, 1.5)
    channel_of = jax.random.permutation(key_list[5], CH).astype(jnp.int32)
    m_orders = draw_m_orders(jax.random.fold_in(key_list[9], 71), 0)
    cycle_of = jax.random.permutation(key_list[7], R_TOT).astype(jnp.int32)
    cycle_pixels = draw_cycle_pixels(jax.random.fold_in(key_list[9], 71), 0)
    return {"comp_alms": comp_alms, "legendre": legendre, "inv_noise": inv_noise, "beam_window": beam_window, "mixing": mixing, "channel_of": channel_of, "m_orders": m_orders, "cycle_of": cycle_of, "cycle_pixels": cycle_pixels}


def phase_rows(orders, pix_count, cycle_width):
    columns = jnp.arange(cycle_width, dtype=jnp.int32)
    phase_steps = (orders[:, None] * (2 * columns[None, :] + 1)) % (2 * pix_count)
    angles = phase_steps.astype(jnp.float32) * (jnp.float32(math.pi) / pix_count.astype(jnp.float32))
    return jnp.concatenate([jnp.cos(angles), jnp.sin(angles)], axis=0).astype(jnp.bfloat16)


def combine_forward(plus_sum, minus_sum):
    return jnp.stack([plus_sum[:, 0] - minus_sum[:, 3], plus_sum[:, 1] + minus_sum[:, 2],
                      plus_sum[:, 2] + minus_sum[:, 1], plus_sum[:, 3] - minus_sum[:, 0]], axis=1)


def twist_grads(cycle_grads):
    return jnp.stack([-cycle_grads[:, 3], cycle_grads[:, 2], cycle_grads[:, 1], -cycle_grads[:, 0]], axis=1)


def cycle_work(coeffs, weights, orders, pix_count):
    slots = coeffs.shape[0]
    cycle_width = weights.shape[-1]
    phases = phase_rows(orders, pix_count, cycle_width)
    half_rows = phases.shape[0] // 2
    real_part = coeffs[:, 0::2]
    imag_part = coeffs[:, 1::2]
    stacked = jnp.concatenate([real_part, -imag_part], axis=2).reshape(2 * slots, 2 * half_rows)
    maps = jnp.dot(stacked, phases, preferred_element_type=jnp.float32)
    live_mask = jnp.arange(cycle_width, dtype=jnp.int32) < pix_count
    scaled = jnp.where(live_mask[None, None, :], weights, 0.0) / pix_count.astype(jnp.float32)
    weighted = (scaled.reshape(maps.shape) * maps).astype(jnp.bfloat16)
    returned = lax.dot_general(weighted, phases, (((1,), (1,)), ((), ())), preferred_element_type=jnp.float32)
    grad_real = returned[:, :half_rows].reshape(slots, 2, half_rows)
    grad_imag = (-returned[:, half_rows:]).reshape(slots, 2, half_rows)
    return jnp.stack([grad_real, grad_imag], axis=2).reshape(slots, 4, half_rows).astype(jnp.bfloat16)


def mix_components(mix_rows, components):
    accum = mix_rows[:, 0, None, None, None] * components[0][None]
    for comp_index in range(1, components.shape[0]):
        accum = accum + mix_rows[:, comp_index, None, None, None] * components[comp_index][None]
    return accum


def reference(comp_alms, legendre, inv_noise, beam_window, mixing, channel_of, m_orders, cycle_of, cycle_pixels):
    length = legendre.shape[2]
    cycle_total = legendre.shape[3]
    mix_rows = jnp.take(mixing, channel_of, axis=0)
    beam_rows = jnp.take(beam_window, channel_of, axis=0)
    keep_mask = (jnp.arange(length, dtype=jnp.int32)[None, :] >= m_orders[:, None]).astype(jnp.float32)
    mixed_alm = mix_components(mix_rows, comp_alms)
    chan_alm = (mixed_alm * beam_rows[:, None, None, :] * keep_mask[None, None]).astype(jnp.bfloat16)
    channels = chan_alm.shape[0]

    def forward_order(index):
        tables = lax.dynamic_index_in_dim(legendre, index, 1, keepdims=False)
        row_block = lax.dynamic_index_in_dim(chan_alm, index, 2, keepdims=False).reshape(channels * 4, length)
        plus_sum = jnp.dot(row_block, tables[0], preferred_element_type=jnp.float32).reshape(channels, 4, cycle_total)
        minus_sum = jnp.dot(row_block, tables[1], preferred_element_type=jnp.float32).reshape(channels, 4, cycle_total)
        return combine_forward(plus_sum, minus_sum)

    cycle_coeffs = lax.map(forward_order, jnp.arange(M_TOT, dtype=jnp.int32))
    cycle_coeffs = jnp.transpose(cycle_coeffs, (1, 2, 0, 3)).astype(jnp.bfloat16)
    slot_coeffs = jnp.take(cycle_coeffs, cycle_of, axis=3)

    def per_cycle(slot):
        coeffs = lax.dynamic_index_in_dim(slot_coeffs, slot, 3, keepdims=False)
        weights = lax.dynamic_index_in_dim(inv_noise, slot, 2, keepdims=False)
        pix_count = cycle_pixels[cycle_of[slot]]
        return cycle_work(coeffs, weights, m_orders, pix_count)

    slot_grads = lax.map(per_cycle, jnp.arange(R_TOT, dtype=jnp.int32))
    slot_grads = jnp.transpose(slot_grads, (1, 2, 3, 0))
    cycle_grads = jnp.zeros_like(slot_grads).at[:, :, :, cycle_of].set(slot_grads)

    def adjoint_order(index):
        tables = lax.dynamic_index_in_dim(legendre, index, 1, keepdims=False)
        order_grads = lax.dynamic_index_in_dim(cycle_grads, index, 2, keepdims=False)
        twisted = twist_grads(order_grads)
        accum = lax.dot_general(order_grads.reshape(channels * 4, cycle_total), tables[0], (((1,), (1,)), ((), ())), preferred_element_type=jnp.float32)
        accum = accum + lax.dot_general(twisted.reshape(channels * 4, cycle_total), tables[1], (((1,), (1,)), ((), ())), preferred_element_type=jnp.float32)
        return accum.reshape(channels, 4, length)

    alm_grads = lax.map(adjoint_order, jnp.arange(M_TOT, dtype=jnp.int32))
    alm_grads = jnp.transpose(alm_grads, (1, 2, 0, 3)) * keep_mask[None, None]
    beamed = alm_grads * beam_rows[:, None, None, :]
    return jnp.einsum('kc,kpml->cpml', mix_rows, beamed, precision=lax.Precision.HIGHEST)
```

```python
import functools
import math

import jax
import jax.numpy as jnp
from jax import lax
from jax.experimental import pallas as pl
from jax.experimental.pallas import tpu as pltpu
from jax.sharding import PartitionSpec as P

F32 = jnp.float32
BF16 = jnp.bfloat16
LANES = 128
NT = (((1,), (1,)), ((), ()))
NN = (((1,), (0,)), ((), ()))


def iota(shape, dim):
    return lax.broadcasted_iota(jnp.int32, shape, dim)


def dot(left, right, dims):
    return lax.dot_general(left, right, dims, preferred_element_type=F32)


def exact_mod(value, modulus, inverse):
    rest = value - jnp.floor(value * inverse) * modulus
    rest = jnp.where(rest < 0, rest + modulus, rest)
    return jnp.where(rest >= modulus, rest - modulus, rest)


def kernel(
    chans, blks, alm_hbm, leg_hbm, inv_hbm, beam_hbm, mix_s, chan_s, order_s, cycle_s, pixel_s,
    cycle_row, out_ref, comp_v, leg_v, inv_v, beam_v, gain_v, slot_leg, phases, send1, recv1,
    send2, recv2, in_sem, send_sem, recv_sem,
):
    comps = comp_v.shape[0]
    shard = comp_v.shape[2]
    cycles = leg_v.shape[1] // 4
    slots = inv_v.shape[0] // 2
    width = inv_v.shape[1]
    rows = 4 * chans
    total = chans * blks
    me_c = lax.axis_index("chan")
    me_b = lax.axis_index("blk")
    first = pl.multiple_of(me_c * shard, shard)

    def peer(offset):
        return lax.rem(me_c + offset // blks, chans), lax.rem(me_b + offset % blks, blks)

    def each_peer(act):
        if total <= 64:
            for offset in range(1, total):
                act(offset)
        else:
            lax.fori_loop(1, total, lambda offset, carry: (act(offset), carry)[1], 0)

    barrier = pltpu.get_barrier_semaphore()

    def greet(offset):
        pl.semaphore_signal(
            barrier, inc=1, device_id=peer(offset), device_id_type=pl.DeviceIdType.MESH
        )

    loads = []

    def load(src, dst):
        copy = pltpu.make_async_copy(src, dst, in_sem.at[len(loads)])
        copy.start()
        loads.append(copy)

    for comp in range(comps):
        for part in range(4):
            for half in range(2):
                load(alm_hbm.at[comp, part], comp_v.at[comp, pl.ds(4 * half + part, 1), :])
    load(beam_hbm.at[:, pl.ds(first, shard)], beam_v)
    for kind in range(2):
        for part in range(4):
            load(
                leg_hbm.at[kind, 0, :, pl.ds(first, shard)],
                leg_v.at[kind, pl.ds(part * cycles, cycles), :],
            )
    early = len(loads)
    for stokes in range(2):
        load(inv_hbm.at[0, stokes], inv_v.at[pl.ds(stokes * slots, slots), :])
    each_peer(greet)
    for copy in loads[:early]:
        copy.wait()

    low_half = iota((8, 1), 0) < 4
    keep = (iota((1, shard), 1) + first >= order_s[me_b]).astype(F32)
    mix_cols = []
    alm_rows = []
    for pair in range(chans // 2):
        picked = [chan_s[2 * pair], chan_s[2 * pair + 1]]
        columns = [
            jnp.where(low_half, mix_s[picked[0], comp], mix_s[picked[1], comp])
            for comp in range(comps)
        ]
        mix_cols.append(columns)
        mixed = columns[0] * comp_v[0]
        for comp in range(1, comps):
            mixed = mixed + columns[comp] * comp_v[comp]
        beam = jnp.where(
            low_half, beam_v[pl.ds(picked[0], 1), :], beam_v[pl.ds(picked[1], 1), :]
        )
        gain = beam * keep
        gain_v[pl.ds(8 * pair, 8), :] = gain
        alm_rows.append(mixed * gain)
    alm = jnp.concatenate(alm_rows, axis=0).astype(BF16)
    plus = dot(alm, leg_v[0], NT)
    minus = dot(alm, leg_v[1], NT)
    row_part = iota(plus.shape, 0) % 4
    lane_part = iota(plus.shape, 1) // cycles
    outer = (lane_part == 0) | (lane_part == 3)
    signed = jnp.where(outer, -minus, minus)
    joined = jnp.where(lane_part == row_part, plus, 0.0) + jnp.where(
        lane_part == 3 - row_part, signed, 0.0
    )
    folded = joined
    for step in range(1, 4):
        folded = folded + pltpu.roll(joined, rows - step, 0)
    send1[...] = folded

    pl.semaphore_wait(barrier, total - 1)

    def scatter(src_of, dst, phase):
        def start(offset):
            dest_c, dest_b = peer(offset)
            pltpu.make_async_remote_copy(
                src_ref=src_of(dest_c, dest_b),
                dst_ref=dst.at[me_c, pl.ds(me_b, 1), :],
                send_sem=send_sem.at[phase, offset],
                recv_sem=recv_sem.at[phase],
                device_id=(dest_c, dest_b),
                device_id_type=pl.DeviceIdType.MESH,
            ).start()

        each_peer(start)
        pltpu.make_async_copy(
            src_of(me_c, me_b), dst.at[me_c, pl.ds(me_b, 1), :], recv_sem.at[phase]
        ).start()

    def arrived(dst, phase):
        pltpu.make_async_copy(dst, dst, recv_sem.at[phase]).wait()

    def sent(src_of, dst, phase):
        def finish(offset):
            dest_c, dest_b = peer(offset)
            pltpu.make_async_remote_copy(
                src_ref=src_of(dest_c, dest_b),
                dst_ref=dst.at[me_c, pl.ds(me_b, 1), :],
                send_sem=send_sem.at[phase, offset],
                recv_sem=recv_sem.at[phase],
                device_id=(dest_c, dest_b),
                device_id_type=pl.DeviceIdType.MESH,
            ).wait_send()

        each_peer(finish)

    def by_channel(dest_c, dest_b):
        return send1.at[pl.ds(4 * dest_c, 1), :]

    def by_order(dest_c, dest_b):
        return send2.at[pl.ds(dest_b, 1), :]

    scatter(by_channel, recv1, 0)

    own_cycles = [cycle_s[me_b * slots + slot] for slot in range(slots)]
    own_pixels = [pixel_s[cycle].astype(F32) for cycle in own_cycles]

    def by_slot(slot_index, values):
        result = jnp.where(slot_index == 0, values[0], values[slots - 1])
        for slot in range(1, slots - 1):
            result = jnp.where(slot_index == slot, values[slot], result)
        return result

    grid = (slots * blks, LANES)
    row = iota(grid, 0)
    lane = iota(grid, 1).astype(F32)
    pixels = by_slot(row // blks, own_pixels)
    orders = jnp.zeros(grid, F32)
    for order in range(blks):
        orders = jnp.where(row % blks == order, order_s[order].astype(F32), orders)
    modulus = 2.0 * pixels
    inverse = 1.0 / modulus
    scale = jnp.float32(math.pi) / pixels
    fine = exact_mod(orders * (2.0 * lane + 1.0), modulus, inverse) * scale
    stride = exact_mod(orders * (2.0 * LANES), modulus, inverse)
    coarse = exact_mod(stride * lane, modulus, inverse) * scale
    fine_cos, fine_sin = jnp.cos(fine), jnp.sin(fine)
    coarse_cos, coarse_sin = jnp.cos(coarse), jnp.sin(coarse)
    half = slots * blks
    for chunk in range(width // LANES):
        turn_cos = coarse_cos[:, chunk : chunk + 1]
        turn_sin = coarse_sin[:, chunk : chunk + 1]
        window = pl.ds(chunk * LANES, LANES)
        phases[pl.ds(0, half), window] = (turn_cos * fine_cos - turn_sin * fine_sin).astype(BF16)
        phases[pl.ds(half, half), window] = (turn_sin * fine_cos + turn_cos * fine_sin).astype(
            BF16
        )

    for copy in loads[early:]:
        copy.wait()
    row_pixels = by_slot(iota((2 * slots, 1), 0) % slots, own_pixels)
    row_inverse = 1.0 / row_pixels
    live = iota((2 * slots, width), 1).astype(F32) < row_pixels
    inv_v[...] = jnp.where(live, inv_v[...], 0.0) * row_inverse

    cycle_hot = (iota((cycles, cycles), 0) == cycle_row[...]).astype(BF16)
    to_row, to_col = iota((cycles, cycles), 0), iota((cycles, cycles), 1)
    reorder = ((to_row // blks == to_col % slots) & (to_row % blks == to_col // slots)).astype(
        F32
    ).astype(BF16)
    slot_hot = dot(reorder, cycle_hot, NT).astype(BF16)
    for kind in range(2):
        slot_leg[pl.ds(kind * cycles, cycles), :] = dot(
            slot_hot, leg_v[kind, pl.ds(0, cycles), :], NN
        ).astype(BF16)

    pick_shape = (2 * slots, 4 * cycles)
    pick_row, pick_lane = iota(pick_shape, 0), iota(pick_shape, 1)
    pick = (
        (pick_lane // (2 * cycles) == pick_row // slots)
        & (pick_lane % cycles == by_slot(pick_row % slots, own_cycles))
    ).astype(F32).astype(BF16)
    place_shape = (2 * slots, 2 * slots * rows)
    place_row, place_lane = iota(place_shape, 0), iota(place_shape, 1)
    lane_p = place_lane % 4
    lane_q = place_lane // rows
    twist = lane_q >= slots
    source_p = jnp.where(twist, 3 - lane_p, lane_p)
    fits = (
        ((place_lane // 4) % chans == me_c)
        & (lane_q % slots == place_row % slots)
        & (source_p // 2 == place_row // slots)
    )
    twist_sign = jnp.where(twist & ((lane_p == 0) | (lane_p == 3)), -1.0, 1.0)
    place = [
        jnp.where(fits & (source_p % 2 == part), twist_sign * (1.0 - 2.0 * part), 0.0).astype(BF16)
        for part in range(2)
    ]

    arrived(recv1, 0)
    coeffs = recv1[0]
    for chan in range(1, chans):
        coeffs = coeffs + recv1[chan]
    even = (iota(coeffs.shape, 1) // cycles) % 2 == 0
    real_block = jnp.where(even, coeffs, 0.0)
    imag_block = jnp.where(even, 0.0, -coeffs)
    spread = jnp.concatenate([real_block] * slots + [imag_block] * slots, axis=0).astype(BF16)
    stacked = dot(pick, spread, NT)
    own_block = (iota(stacked.shape, 1) // blks) % slots == iota(stacked.shape, 0) % slots
    stacked = jnp.where(own_block, stacked, 0.0).astype(BF16)

    piece = min(1024, width)
    grads = jnp.zeros((2 * half, 2 * slots), F32)
    for index in range(width // piece):
        window = pl.ds(index * piece, piece)
        table = phases[:, window]
        maps = dot(stacked, table, NN)
        weighted = (inv_v[:, window] * maps).astype(BF16)
        grads = grads + dot(table, weighted, NT)
    own_lane = (iota(grads.shape, 0) // blks) % slots == iota(grads.shape, 1) % slots
    grads = jnp.where(own_lane, grads, 0.0)
    placed = None
    for part in range(2):
        summed = grads[part * half : part * half + blks]
        for slot in range(1, slots):
            begin = part * half + slot * blks
            summed = summed + grads[begin : begin + blks]
        term = dot(summed.astype(BF16), place[part], NN)
        placed = term if placed is None else placed + term
    send2[...] = placed
    scatter(by_order, recv2, 1)
    sent(by_channel, recv1, 0)

    arrived(recv2, 1)
    returned = recv2[0]
    for chan in range(1, chans):
        returned = returned + recv2[chan]
    lanes = returned.shape[1]
    blocks = [returned] + [
        pltpu.roll(returned, lanes - index * rows, 1) for index in range(1, 2 * slots)
    ]
    turned = jnp.concatenate(blocks, axis=0)[:, : max(rows, LANES)].T
    alm_grads = dot(turned[:rows].astype(BF16), slot_leg[...], NN) * gain_v[...]
    for comp in range(comps):
        mixed = mix_cols[0][comp] * alm_grads[0:8]
        for pair in range(1, chans // 2):
            mixed = mixed + mix_cols[pair][comp] * alm_grads[8 * pair : 8 * pair + 8]
        out_ref[comp] = mixed[0:4] + mixed[4:8]
    sent(by_order, recv2, 1)


def body(
    chans, blks, comp_alms, legendre, inv_noise, beam_window, mixing, channel_of, m_orders,
    cycle_of, cycle_pixels,
):
    comps, parts, order_dev, shard = comp_alms.shape
    cycles = legendre.shape[3]
    chan_dev, stokes, slots, width = inv_noise.shape
    assert parts == 4 and stokes == 2 and order_dev == 1 and chan_dev == 1
    rows = 4 * chans
    any_space = pl.BlockSpec(memory_space=pl.ANY)
    scalars = pl.BlockSpec(memory_space=pltpu.SMEM)
    vector = pl.BlockSpec(memory_space=pltpu.VMEM)
    lanes2 = 2 * slots * rows
    result = pl.pallas_call(
        functools.partial(kernel, chans, blks),
        out_shape=jax.ShapeDtypeStruct((comps, 4, shard), F32),
        in_specs=[any_space] * 4 + [scalars] * 5 + [vector],
        out_specs=vector,
        scratch_shapes=[
            pltpu.VMEM((comps, 8, shard), F32),
            pltpu.VMEM((2, 4 * cycles, shard), BF16),
            pltpu.VMEM((2 * slots, width), F32),
            pltpu.VMEM((beam_window.shape[0], shard), F32),
            pltpu.VMEM((rows, shard), F32),
            pltpu.VMEM((2 * cycles, shard), BF16),
            pltpu.VMEM((2 * slots * blks, width), BF16),
            pltpu.VMEM((rows, 4 * cycles), F32),
            pltpu.VMEM((chans, blks, 4 * cycles), F32),
            pltpu.VMEM((blks, lanes2), F32),
            pltpu.VMEM((chans, blks, lanes2), F32),
            pltpu.SemaphoreType.DMA((comps * 8 + 11,)),
            pltpu.SemaphoreType.DMA((2, chans * blks)),
            pltpu.SemaphoreType.DMA((2,)),
        ],
        compiler_params=pltpu.CompilerParams(collective_id=0, has_side_effects=True),
        name="normal_product",
    )(
        comp_alms, jnp.swapaxes(legendre, 2, 3), inv_noise, beam_window, mixing, channel_of,
        m_orders, cycle_of, cycle_pixels, cycle_of.reshape(1, cycles),
    )
    return result.reshape(comp_alms.shape)


def solution(mesh):
    in_specs = (
        P(None, None, "blk", "chan"),
        P(None, "blk", None, None),
        P("chan", None, "blk", None),
        P(),
        P(),
        P(),
        P(),
        P(),
        P(),
    )
    out_specs = P(None, None, "blk", "chan")
    work = functools.partial(body, mesh.shape["chan"], mesh.shape["blk"])
    return jax.shard_map(work, mesh=mesh, in_specs=in_specs, out_specs=out_specs, check_vma=False)
```

```python
import functools
import math

import jax
import jax.numpy as jnp
from jax import lax
from jax.experimental import pallas as pl
from jax.experimental.pallas import tpu as pltpu
from jax.sharding import PartitionSpec as P

F32 = jnp.float32
BF16 = jnp.bfloat16
LANES = 128
NT = (((1,), (1,)), ((), ()))
NN = (((1,), (0,)), ((), ()))


def iota(shape, dim):
    return lax.broadcasted_iota(jnp.int32, shape, dim)


def dot(left, right, dims):
    return lax.dot_general(left, right, dims, preferred_element_type=F32)


def exact_mod(value, modulus, inverse):
    rest = value - jnp.floor(value * inverse) * modulus
    rest = jnp.where(rest < 0, rest + modulus, rest)
    return jnp.where(rest >= modulus, rest - modulus, rest)


def kernel(
    chans, blks, alm_hbm, leg_hbm, inv_hbm, beam_hbm, mix_hbm, chan_hbm, order_hbm, cycle_hbm,
    pixel_hbm, cycle_row_hbm, out_ref, mix_s, chan_s, order_s, cycle_s, pixel_s, cycle_row, comp_v,
    leg_v, inv_v, beam_v, gain_v, slot_leg, phases, send1, recv1, send2, recv2, in_sem, send_sem,
    recv_sem,
):
    comps = comp_v.shape[0]
    shard = comp_v.shape[2]
    cycles = leg_v.shape[1] // 4
    slots = inv_v.shape[0] // 2
    width = inv_v.shape[1]
    rows = 4 * chans
    total = chans * blks
    me_c = lax.axis_index("chan")
    me_b = lax.axis_index("blk")
    first = pl.multiple_of(me_c * shard, shard)

    def peer(offset):
        return lax.rem(me_c + offset // blks, chans), lax.rem(me_b + offset % blks, blks)

    def each_peer(act):
        if total <= 64:
            for offset in range(1, total):
                act(offset)
        else:
            lax.fori_loop(1, total, lambda offset, carry: (act(offset), carry)[1], 0)

    barrier = pltpu.get_barrier_semaphore()

    def greet(offset):
        pl.semaphore_signal(
            barrier, inc=1, device_id=peer(offset), device_id_type=pl.DeviceIdType.MESH
        )

    each_peer(greet)
    loads = []

    def load(src, dst):
        copy = pltpu.make_async_copy(src, dst, in_sem.at[len(loads)])
        copy.start()
        loads.append(copy)

    for src, dst in (
        (mix_hbm, mix_s), (chan_hbm, chan_s), (order_hbm, order_s), (cycle_hbm, cycle_s),
        (pixel_hbm, pixel_s), (cycle_row_hbm, cycle_row),
    ):
        load(src, dst)
    for comp in range(comps):
        for part in range(4):
            for half in range(2):
                load(alm_hbm.at[comp, part], comp_v.at[comp, pl.ds(4 * half + part, 1), :])
    load(beam_hbm.at[:, pl.ds(first, shard)], beam_v)
    for kind in range(2):
        for part in range(4):
            load(
                leg_hbm.at[kind, 0, :, pl.ds(first, shard)],
                leg_v.at[kind, pl.ds(part * cycles, cycles), :],
            )
    early = len(loads)
    for stokes in range(2):
        load(inv_hbm.at[0, stokes], inv_v.at[pl.ds(stokes * slots, slots), :])
    for copy in loads[:early]:
        copy.wait()

    low_half = iota((8, 1), 0) < 4
    keep = (iota((1, shard), 1) + first >= order_s[me_b]).astype(F32)
    mix_cols = []
    alm_rows = []
    for pair in range(chans // 2):
        picked = [chan_s[2 * pair], chan_s[2 * pair + 1]]
        columns = [
            jnp.where(low_half, mix_s[picked[0], comp], mix_s[picked[1], comp])
            for comp in range(comps)
        ]
        mix_cols.append(columns)
        mixed = columns[0] * comp_v[0]
        for comp in range(1, comps):
            mixed = mixed + columns[comp] * comp_v[comp]
        beam = jnp.where(
            low_half, beam_v[pl.ds(picked[0], 1), :], beam_v[pl.ds(picked[1], 1), :]
        )
        gain = beam * keep
        gain_v[pl.ds(8 * pair, 8), :] = gain
        alm_rows.append(mixed * gain)
    alm = jnp.concatenate(alm_rows, axis=0).astype(BF16)
    plus = dot(alm, leg_v[0], NT)
    minus = dot(alm, leg_v[1], NT)
    row_part = iota(plus.shape, 0) % 4
    lane_part = iota(plus.shape, 1) // cycles
    outer = (lane_part == 0) | (lane_part == 3)
    signed = jnp.where(outer, -minus, minus)
    joined = jnp.where(lane_part == row_part, plus, 0.0) + jnp.where(
        lane_part == 3 - row_part, signed, 0.0
    )
    folded = joined
    for step in range(1, 4):
        folded = folded + pltpu.roll(joined, rows - step, 0)
    send1[...] = folded

    pl.semaphore_wait(barrier, total - 1)

    def scatter(src_of, dst, phase):
        def start(offset):
            dest_c, dest_b = peer(offset)
            pltpu.make_async_remote_copy(
                src_ref=src_of(dest_c, dest_b),
                dst_ref=dst.at[me_c, pl.ds(me_b, 1), :],
                send_sem=send_sem.at[phase, offset],
                recv_sem=recv_sem.at[phase],
                device_id=(dest_c, dest_b),
                device_id_type=pl.DeviceIdType.MESH,
            ).start()

        each_peer(start)
        pltpu.make_async_copy(
            src_of(me_c, me_b), dst.at[me_c, pl.ds(me_b, 1), :], recv_sem.at[phase]
        ).start()

    def arrived(dst, phase):
        pltpu.make_async_copy(dst, dst, recv_sem.at[phase]).wait()

    def sent(src_of, dst, phase):
        def finish(offset):
            dest_c, dest_b = peer(offset)
            pltpu.make_async_remote_copy(
                src_ref=src_of(dest_c, dest_b),
                dst_ref=dst.at[me_c, pl.ds(me_b, 1), :],
                send_sem=send_sem.at[phase, offset],
                recv_sem=recv_sem.at[phase],
                device_id=(dest_c, dest_b),
                device_id_type=pl.DeviceIdType.MESH,
            ).wait_send()

        each_peer(finish)

    def by_channel(dest_c, dest_b):
        return send1.at[pl.ds(4 * dest_c, 1), :]

    def by_order(dest_c, dest_b):
        return send2.at[pl.ds(dest_b, 1), :]

    scatter(by_channel, recv1, 0)

    own_cycles = [cycle_s[me_b * slots + slot] for slot in range(slots)]
    own_pixels = [pixel_s[cycle].astype(F32) for cycle in own_cycles]

    def by_slot(slot_index, values):
        result = jnp.where(slot_index == 0, values[0], values[slots - 1])
        for slot in range(1, slots - 1):
            result = jnp.where(slot_index == slot, values[slot], result)
        return result

    grid = (slots * blks, LANES)
    row = iota(grid, 0)
    lane = iota(grid, 1).astype(F32)
    pixels = by_slot(row // blks, own_pixels)
    orders = jnp.zeros(grid, F32)
    for order in range(blks):
        orders = jnp.where(row % blks == order, order_s[order].astype(F32), orders)
    modulus = 2.0 * pixels
    inverse = 1.0 / modulus
    scale = jnp.float32(math.pi) / pixels
    fine = exact_mod(orders * (2.0 * lane + 1.0), modulus, inverse) * scale
    stride = exact_mod(orders * (2.0 * LANES), modulus, inverse)
    coarse = exact_mod(stride * lane, modulus, inverse) * scale
    fine_cos, fine_sin = jnp.cos(fine), jnp.sin(fine)
    coarse_cos, coarse_sin = jnp.cos(coarse), jnp.sin(coarse)
    half = slots * blks
    for chunk in range(width // LANES):
        turn_cos = coarse_cos[:, chunk : chunk + 1]
        turn_sin = coarse_sin[:, chunk : chunk + 1]
        window = pl.ds(chunk * LANES, LANES)
        phases[pl.ds(0, half), window] = (turn_cos * fine_cos - turn_sin * fine_sin).astype(BF16)
        phases[pl.ds(half, half), window] = (turn_sin * fine_cos + turn_cos * fine_sin).astype(
            BF16
        )

    for copy in loads[early:]:
        copy.wait()
    row_pixels = by_slot(iota((2 * slots, 1), 0) % slots, own_pixels)
    row_inverse = 1.0 / row_pixels
    live = iota((2 * slots, width), 1).astype(F32) < row_pixels
    inv_v[...] = jnp.where(live, inv_v[...], 0.0) * row_inverse

    cycle_hot = (iota((cycles, cycles), 0) == cycle_row[...]).astype(BF16)
    to_row, to_col = iota((cycles, cycles), 0), iota((cycles, cycles), 1)
    reorder = ((to_row // blks == to_col % slots) & (to_row % blks == to_col // slots)).astype(
        F32
    ).astype(BF16)
    slot_hot = dot(reorder, cycle_hot, NT).astype(BF16)
    for kind in range(2):
        slot_leg[pl.ds(kind * cycles, cycles), :] = dot(
            slot_hot, leg_v[kind, pl.ds(0, cycles), :], NN
        ).astype(BF16)

    pick_shape = (2 * slots, 4 * cycles)
    pick_row, pick_lane = iota(pick_shape, 0), iota(pick_shape, 1)
    pick = (
        (pick_lane // (2 * cycles) == pick_row // slots)
        & (pick_lane % cycles == by_slot(pick_row % slots, own_cycles))
    ).astype(F32).astype(BF16)
    place_shape = (2 * slots, 2 * slots * rows)
    place_row, place_lane = iota(place_shape, 0), iota(place_shape, 1)
    lane_p = place_lane % 4
    lane_q = place_lane // rows
    twist = lane_q >= slots
    source_p = jnp.where(twist, 3 - lane_p, lane_p)
    fits = (
        ((place_lane // 4) % chans == me_c)
        & (lane_q % slots == place_row % slots)
        & (source_p // 2 == place_row // slots)
    )
    twist_sign = jnp.where(twist & ((lane_p == 0) | (lane_p == 3)), -1.0, 1.0)
    place = [
        jnp.where(fits & (source_p % 2 == part), twist_sign * (1.0 - 2.0 * part), 0.0).astype(BF16)
        for part in range(2)
    ]

    arrived(recv1, 0)
    coeffs = recv1[0]
    for chan in range(1, chans):
        coeffs = coeffs + recv1[chan]
    even = (iota(coeffs.shape, 1) // cycles) % 2 == 0
    real_block = jnp.where(even, coeffs, 0.0)
    imag_block = jnp.where(even, 0.0, -coeffs)
    spread = jnp.concatenate([real_block] * slots + [imag_block] * slots, axis=0).astype(BF16)
    stacked = dot(pick, spread, NT)
    own_block = (iota(stacked.shape, 1) // blks) % slots == iota(stacked.shape, 0) % slots
    stacked = jnp.where(own_block, stacked, 0.0).astype(BF16)

    piece = min(1024, width)
    grads = jnp.zeros((2 * half, 2 * slots), F32)
    for index in range(width // piece):
        window = pl.ds(index * piece, piece)
        table = phases[:, window]
        maps = dot(stacked, table, NN)
        weighted = (inv_v[:, window] * maps).astype(BF16)
        grads = grads + dot(table, weighted, NT)
    own_lane = (iota(grads.shape, 0) // blks) % slots == iota(grads.shape, 1) % slots
    grads = jnp.where(own_lane, grads, 0.0)
    placed = None
    for part in range(2):
        summed = grads[part * half : part * half + blks]
        for slot in range(1, slots):
            begin = part * half + slot * blks
            summed = summed + grads[begin : begin + blks]
        term = dot(summed.astype(BF16), place[part], NN)
        placed = term if placed is None else placed + term
    send2[...] = placed
    scatter(by_order, recv2, 1)
    sent(by_channel, recv1, 0)

    arrived(recv2, 1)
    returned = recv2[0]
    for chan in range(1, chans):
        returned = returned + recv2[chan]
    lanes = returned.shape[1]
    blocks = [returned] + [
        pltpu.roll(returned, lanes - index * rows, 1) for index in range(1, 2 * slots)
    ]
    turned = jnp.concatenate(blocks, axis=0)[:, : max(rows, LANES)].T
    alm_grads = dot(turned[:rows].astype(BF16), slot_leg[...], NN) * gain_v[...]
    for comp in range(comps):
        mixed = mix_cols[0][comp] * alm_grads[0:8]
        for pair in range(1, chans // 2):
            mixed = mixed + mix_cols[pair][comp] * alm_grads[8 * pair : 8 * pair + 8]
        out_ref[comp] = mixed[0:4] + mixed[4:8]
    sent(by_order, recv2, 1)


def body(
    chans, blks, comp_alms, legendre, inv_noise, beam_window, mixing, channel_of, m_orders,
    cycle_of, cycle_pixels,
):
    comps, parts, order_dev, shard = comp_alms.shape
    cycles = legendre.shape[3]
    chan_dev, stokes, slots, width = inv_noise.shape
    assert parts == 4 and stokes == 2 and order_dev == 1 and chan_dev == 1
    rows = 4 * chans
    any_space = pl.BlockSpec(memory_space=pl.ANY)
    vector = pl.BlockSpec(memory_space=pltpu.VMEM)
    lanes2 = 2 * slots * rows
    result = pl.pallas_call(
        functools.partial(kernel, chans, blks),
        out_shape=pltpu.VMEM((comps, 4, shard), F32),
        in_specs=[any_space] * 10,
        out_specs=vector,
        scratch_shapes=[
            pltpu.SMEM(mixing.shape, F32),
            pltpu.SMEM(channel_of.shape, jnp.int32),
            pltpu.SMEM(m_orders.shape, jnp.int32),
            pltpu.SMEM(cycle_of.shape, jnp.int32),
            pltpu.SMEM(cycle_pixels.shape, jnp.int32),
            pltpu.VMEM((1, cycles), jnp.int32),
            pltpu.VMEM((comps, 8, shard), F32),
            pltpu.VMEM((2, 4 * cycles, shard), BF16),
            pltpu.VMEM((2 * slots, width), F32),
            pltpu.VMEM((beam_window.shape[0], shard), F32),
            pltpu.VMEM((rows, shard), F32),
            pltpu.VMEM((2 * cycles, shard), BF16),
            pltpu.VMEM((2 * slots * blks, width), BF16),
            pltpu.VMEM((rows, 4 * cycles), F32),
            pltpu.VMEM((chans, blks, 4 * cycles), F32),
            pltpu.VMEM((blks, lanes2), F32),
            pltpu.VMEM((chans, blks, lanes2), F32),
            pltpu.SemaphoreType.DMA((comps * 8 + 17,)),
            pltpu.SemaphoreType.DMA((2, chans * blks)),
            pltpu.SemaphoreType.DMA((2,)),
        ],
        compiler_params=pltpu.CompilerParams(collective_id=0, has_side_effects=True),
        name="normal_product",
    )(
        comp_alms, jnp.swapaxes(legendre, 2, 3), inv_noise, beam_window, mixing, channel_of,
        m_orders, cycle_of, cycle_pixels, cycle_of.reshape(1, cycles),
    )
    return result.reshape(comp_alms.shape)


def solution(mesh):
    in_specs = (
        P(None, None, "blk", "chan"),
        P(None, "blk", None, None),
        P("chan", None, "blk", None),
        P(),
        P(),
        P(),
        P(),
        P(),
        P(),
    )
    out_specs = P(None, None, "blk", "chan")
    work = functools.partial(body, mesh.shape["chan"], mesh.shape["blk"])
    return jax.shard_map(work, mesh=mesh, in_specs=in_specs, out_specs=out_specs, check_vma=False)
```

```python
import functools
import math

import jax
import jax.numpy as jnp
from jax import lax
from jax.experimental import pallas as pl
from jax.experimental.pallas import tpu as pltpu
from jax.sharding import PartitionSpec as P

F32 = jnp.float32
BF16 = jnp.bfloat16
LANES = 128
NT = (((1,), (1,)), ((), ()))
NN = (((1,), (0,)), ((), ()))


def iota(shape, dim):
    return lax.broadcasted_iota(jnp.int32, shape, dim)


def dot(left, right, dims):
    return lax.dot_general(left, right, dims, preferred_element_type=F32)


def exact_mod(value, modulus, inverse):
    rest = value - jnp.floor(value * inverse) * modulus
    rest = jnp.where(rest < 0, rest + modulus, rest)
    return jnp.where(rest >= modulus, rest - modulus, rest)


def kernel(
    chans, blks, alm_hbm, leg_hbm, inv_hbm, beam_hbm, mix_hbm, chan_hbm, order_hbm, cycle_hbm,
    pixel_hbm, cycle_row_hbm, out_ref, mix_s, chan_s, order_s, cycle_s, pixel_s, cycle_row, comp_v,
    leg_v, inv_v, beam_v, gain_v, slot_leg, phases, send1, recv1, send2, recv2, spare, in_sem, send_sem,
    recv_sem,
):
    comps = comp_v.shape[0]
    shard = comp_v.shape[2]
    cycles = leg_v.shape[1] // 4
    slots = inv_v.shape[0] // 2
    width = inv_v.shape[1]
    rows = 4 * chans
    total = chans * blks
    me_c = lax.axis_index("chan")
    me_b = lax.axis_index("blk")
    first = pl.multiple_of(me_c * shard, shard)

    def peer(offset):
        return lax.rem(me_c + offset // blks, chans), lax.rem(me_b + offset % blks, blks)

    def each_peer(act):
        if total <= 64:
            for offset in range(1, total):
                act(offset)
        else:
            lax.fori_loop(1, total, lambda offset, carry: (act(offset), carry)[1], 0)

    barrier = pltpu.get_barrier_semaphore()

    def greet(offset):
        pl.semaphore_signal(
            barrier, inc=1, device_id=peer(offset), device_id_type=pl.DeviceIdType.MESH
        )

    each_peer(greet)
    scalars = []

    def load(src, dst, group):
        copy = pltpu.make_async_copy(src, dst, in_sem.at[group])
        copy.start()
        return copy

    def loaded(dst, group):
        pltpu.make_async_copy(dst, dst, in_sem.at[group]).wait()

    for src, dst in (
        (mix_hbm, mix_s), (chan_hbm, chan_s), (order_hbm, order_s), (cycle_hbm, cycle_s),
        (pixel_hbm, pixel_s), (cycle_row_hbm, cycle_row),
    ):
        scalars.append(load(src, dst, 4 + len(scalars)))
    for comp in range(comps):
        for part in range(4):
            for half in range(2):
                load(alm_hbm.at[comp, part], comp_v.at[comp, pl.ds(4 * half + part, 1), :], 0)
    load(beam_hbm.at[:, pl.ds(first, shard)], beam_v, 1)
    for kind in range(2):
        for part in range(4):
            load(
                leg_hbm.at[kind, 0, :, pl.ds(first, shard)],
                leg_v.at[kind, pl.ds(part * cycles, cycles), :],
                2,
            )
    for stokes in range(2):
        load(inv_hbm.at[0, stokes], inv_v.at[pl.ds(stokes * slots, slots), :], 3)
    for copy in scalars:
        copy.wait()
    loaded(comp_v, 0)
    loaded(beam_v, 1)
    loaded(leg_v, 2)

    low_half = iota((8, 1), 0) < 4
    keep = (iota((1, shard), 1) + first >= order_s[me_b]).astype(F32)
    mix_cols = []
    alm_rows = []
    for pair in range(chans // 2):
        picked = [chan_s[2 * pair], chan_s[2 * pair + 1]]
        columns = [
            jnp.where(low_half, mix_s[picked[0], comp], mix_s[picked[1], comp])
            for comp in range(comps)
        ]
        mix_cols.append(columns)
        mixed = columns[0] * comp_v[0]
        for comp in range(1, comps):
            mixed = mixed + columns[comp] * comp_v[comp]
        beam = jnp.where(
            low_half, beam_v[pl.ds(picked[0], 1), :], beam_v[pl.ds(picked[1], 1), :]
        )
        gain = beam * keep
        gain_v[pl.ds(8 * pair, 8), :] = gain
        alm_rows.append(mixed * gain)
    alm = jnp.concatenate(alm_rows, axis=0).astype(BF16)
    plus = dot(alm, leg_v[0], NT)
    minus = dot(alm, leg_v[1], NT)
    row_part = iota(plus.shape, 0) % 4
    lane_part = iota(plus.shape, 1) // cycles
    outer = (lane_part == 0) | (lane_part == 3)
    signed = jnp.where(outer, -minus, minus)
    joined = jnp.where(lane_part == row_part, plus, 0.0) + jnp.where(
        lane_part == 3 - row_part, signed, 0.0
    )
    folded = joined
    for step in range(1, 4):
        folded = folded + pltpu.roll(joined, rows - step, 0)
    send1[...] = folded

    pl.semaphore_wait(barrier, total - 1)

    def scatter(src_of, dst, phase):
        def start(offset):
            dest_c, dest_b = peer(offset)
            pltpu.make_async_remote_copy(
                src_ref=src_of(dest_c, dest_b),
                dst_ref=dst.at[me_c, pl.ds(me_b, 1), :],
                send_sem=send_sem.at[phase],
                recv_sem=recv_sem.at[phase],
                device_id=(dest_c, dest_b),
                device_id_type=pl.DeviceIdType.MESH,
            ).start()

        each_peer(start)
        pltpu.make_async_copy(
            src_of(me_c, me_b), dst.at[me_c, pl.ds(me_b, 1), :], recv_sem.at[phase]
        ).start()
        pltpu.make_async_copy(src_of(me_c, me_b), spare.at[phase], send_sem.at[phase]).start()

    def arrived(dst, phase):
        pltpu.make_async_copy(dst, dst, recv_sem.at[phase]).wait()

    def sent(dst, phase):
        pltpu.make_async_copy(dst, dst, send_sem.at[phase]).wait()

    def by_channel(dest_c, dest_b):
        return send1.at[pl.ds(4 * dest_c, 1), :]

    def by_order(dest_c, dest_b):
        return send2.at[pl.ds(dest_b, 1), :]

    scatter(by_channel, recv1, 0)

    own_cycles = [cycle_s[me_b * slots + slot] for slot in range(slots)]
    own_pixels = [pixel_s[cycle].astype(F32) for cycle in own_cycles]

    def by_slot(slot_index, values):
        result = jnp.where(slot_index == 0, values[0], values[slots - 1])
        for slot in range(1, slots - 1):
            result = jnp.where(slot_index == slot, values[slot], result)
        return result

    grid = (slots * blks, LANES)
    row = iota(grid, 0)
    lane = iota(grid, 1).astype(F32)
    pixels = by_slot(row // blks, own_pixels)
    orders = jnp.zeros(grid, F32)
    for order in range(blks):
        orders = jnp.where(row % blks == order, order_s[order].astype(F32), orders)
    modulus = 2.0 * pixels
    inverse = 1.0 / modulus
    scale = jnp.float32(math.pi) / pixels
    fine = exact_mod(orders * (2.0 * lane + 1.0), modulus, inverse) * scale
    stride = exact_mod(orders * (2.0 * LANES), modulus, inverse)
    coarse = exact_mod(stride * lane, modulus, inverse) * scale
    fine_cos, fine_sin = jnp.cos(fine), jnp.sin(fine)
    coarse_cos, coarse_sin = jnp.cos(coarse), jnp.sin(coarse)
    half = slots * blks
    for chunk in range(width // LANES):
        turn_cos = coarse_cos[:, chunk : chunk + 1]
        turn_sin = coarse_sin[:, chunk : chunk + 1]
        window = pl.ds(chunk * LANES, LANES)
        phases[pl.ds(0, half), window] = (turn_cos * fine_cos - turn_sin * fine_sin).astype(BF16)
        phases[pl.ds(half, half), window] = (turn_sin * fine_cos + turn_cos * fine_sin).astype(
            BF16
        )

    loaded(inv_v, 3)
    row_pixels = by_slot(iota((2 * slots, 1), 0) % slots, own_pixels)
    row_inverse = 1.0 / row_pixels
    live = iota((2 * slots, width), 1).astype(F32) < row_pixels
    inv_v[...] = jnp.where(live, inv_v[...], 0.0) * row_inverse

    cycle_hot = (iota((cycles, cycles), 0) == cycle_row[...]).astype(BF16)
    to_row, to_col = iota((cycles, cycles), 0), iota((cycles, cycles), 1)
    reorder = ((to_row // blks == to_col % slots) & (to_row % blks == to_col // slots)).astype(
        F32
    ).astype(BF16)
    slot_hot = dot(reorder, cycle_hot, NT).astype(BF16)
    for kind in range(2):
        slot_leg[pl.ds(kind * cycles, cycles), :] = dot(
            slot_hot, leg_v[kind, pl.ds(0, cycles), :], NN
        ).astype(BF16)

    pick_shape = (2 * slots, 4 * cycles)
    pick_row, pick_lane = iota(pick_shape, 0), iota(pick_shape, 1)
    pick = (
        (pick_lane // (2 * cycles) == pick_row // slots)
        & (pick_lane % cycles == by_slot(pick_row % slots, own_cycles))
    ).astype(F32).astype(BF16)
    place_shape = (2 * slots, 2 * slots * rows)
    place_row, place_lane = iota(place_shape, 0), iota(place_shape, 1)
    lane_p = place_lane % 4
    lane_q = place_lane // rows
    twist = lane_q >= slots
    source_p = jnp.where(twist, 3 - lane_p, lane_p)
    fits = (
        ((place_lane // 4) % chans == me_c)
        & (lane_q % slots == place_row % slots)
        & (source_p // 2 == place_row // slots)
    )
    twist_sign = jnp.where(twist & ((lane_p == 0) | (lane_p == 3)), -1.0, 1.0)
    place = [
        jnp.where(fits & (source_p % 2 == part), twist_sign * (1.0 - 2.0 * part), 0.0).astype(BF16)
        for part in range(2)
    ]

    arrived(recv1, 0)
    coeffs = recv1[0]
    for chan in range(1, chans):
        coeffs = coeffs + recv1[chan]
    even = (iota(coeffs.shape, 1) // cycles) % 2 == 0
    real_block = jnp.where(even, coeffs, 0.0)
    imag_block = jnp.where(even, 0.0, -coeffs)
    spread = jnp.concatenate([real_block] * slots + [imag_block] * slots, axis=0).astype(BF16)
    stacked = dot(pick, spread, NT)
    own_block = (iota(stacked.shape, 1) // blks) % slots == iota(stacked.shape, 0) % slots
    stacked = jnp.where(own_block, stacked, 0.0).astype(BF16)

    piece = min(1024, width)
    grads = jnp.zeros((2 * half, 2 * slots), F32)
    for index in range(width // piece):
        window = pl.ds(index * piece, piece)
        table = phases[:, window]
        maps = dot(stacked, table, NN)
        weighted = (inv_v[:, window] * maps).astype(BF16)
        grads = grads + dot(table, weighted, NT)
    own_lane = (iota(grads.shape, 0) // blks) % slots == iota(grads.shape, 1) % slots
    grads = jnp.where(own_lane, grads, 0.0)
    placed = None
    for part in range(2):
        summed = grads[part * half : part * half + blks]
        for slot in range(1, slots):
            begin = part * half + slot * blks
            summed = summed + grads[begin : begin + blks]
        term = dot(summed.astype(BF16), place[part], NN)
        placed = term if placed is None else placed + term
    send2[...] = placed
    scatter(by_order, recv2, 1)
    sent(recv1, 0)

    arrived(recv2, 1)
    returned = recv2[0]
    for chan in range(1, chans):
        returned = returned + recv2[chan]
    lanes = returned.shape[1]
    blocks = [returned] + [
        pltpu.roll(returned, lanes - index * rows, 1) for index in range(1, 2 * slots)
    ]
    turned = jnp.concatenate(blocks, axis=0)[:, : max(rows, LANES)].T
    alm_grads = dot(turned[:rows].astype(BF16), slot_leg[...], NN) * gain_v[...]
    for comp in range(comps):
        mixed = mix_cols[0][comp] * alm_grads[0:8]
        for pair in range(1, chans // 2):
            mixed = mixed + mix_cols[pair][comp] * alm_grads[8 * pair : 8 * pair + 8]
        out_ref[comp] = mixed[0:4] + mixed[4:8]
    sent(recv2, 1)


def body(
    chans, blks, comp_alms, legendre, inv_noise, beam_window, mixing, channel_of, m_orders,
    cycle_of, cycle_pixels,
):
    comps, parts, order_dev, shard = comp_alms.shape
    cycles = legendre.shape[3]
    chan_dev, stokes, slots, width = inv_noise.shape
    assert parts == 4 and stokes == 2 and order_dev == 1 and chan_dev == 1
    rows = 4 * chans
    any_space = pl.BlockSpec(memory_space=pl.ANY)
    vector = pl.BlockSpec(memory_space=pltpu.VMEM)
    lanes2 = 2 * slots * rows
    assert lanes2 == 4 * cycles
    result = pl.pallas_call(
        functools.partial(kernel, chans, blks),
        out_shape=pltpu.VMEM((comps, 4, shard), F32),
        in_specs=[any_space] * 10,
        out_specs=vector,
        scratch_shapes=[
            pltpu.SMEM(mixing.shape, F32),
            pltpu.SMEM(channel_of.shape, jnp.int32),
            pltpu.SMEM(m_orders.shape, jnp.int32),
            pltpu.SMEM(cycle_of.shape, jnp.int32),
            pltpu.SMEM(cycle_pixels.shape, jnp.int32),
            pltpu.VMEM((1, cycles), jnp.int32),
            pltpu.VMEM((comps, 8, shard), F32),
            pltpu.VMEM((2, 4 * cycles, shard), BF16),
            pltpu.VMEM((2 * slots, width), F32),
            pltpu.VMEM((beam_window.shape[0], shard), F32),
            pltpu.VMEM((rows, shard), F32),
            pltpu.VMEM((2 * cycles, shard), BF16),
            pltpu.VMEM((2 * slots * blks, width), BF16),
            pltpu.VMEM((rows, 4 * cycles), F32),
            pltpu.VMEM((chans, blks, 4 * cycles), F32),
            pltpu.VMEM((blks, lanes2), F32),
            pltpu.VMEM((chans, blks, lanes2), F32),
            pltpu.VMEM((2, 1, 4 * cycles), F32),
            pltpu.SemaphoreType.DMA((10,)),
            pltpu.SemaphoreType.DMA((2,)),
            pltpu.SemaphoreType.DMA((2,)),
        ],
        compiler_params=pltpu.CompilerParams(collective_id=0, has_side_effects=True),
        name="normal_product",
    )(
        comp_alms, jnp.swapaxes(legendre, 2, 3), inv_noise, beam_window, mixing, channel_of,
        m_orders, cycle_of, cycle_pixels, cycle_of.reshape(1, cycles),
    )
    return result.reshape(comp_alms.shape)


def solution(mesh):
    in_specs = (
        P(None, None, "blk", "chan"),
        P(None, "blk", None, None),
        P("chan", None, "blk", None),
        P(),
        P(),
        P(),
        P(),
        P(),
        P(),
    )
    out_specs = P(None, None, "blk", "chan")
    work = functools.partial(body, mesh.shape["chan"], mesh.shape["blk"])
    return jax.shard_map(work, mesh=mesh, in_specs=in_specs, out_specs=out_specs, check_vma=False)
```
